128 devices in a mesh: dp: 4 (over x), row: 4 (over z_hi, core), col: 8 (over y, z_lo).
Axes of the slice: x: 4, y: 4, z: 4 (z_hi: 2, z_lo: 2; z = z_hi * 2 + z_lo), core: 2. Of those that a mesh axis runs over, the one named last changes fastest.
Arguments:
- activation: bfloat16 [2048, 16384], P('dp', ('row', 'col')), may hold values from -50 to 50
- weight: bfloat16 [8192, 16384], P(('dp', 'col'), 'row'), may hold values from -6 to 6
- prune_mask: int32 [8192, 128], P(('dp', 'col')), may hold values 0 or 1
- channel_rank: int32 [128], replicated, may hold values from 0 to 127, each once
Outputs:
- pruned_weight: bfloat16 [8192, 16384], P(('dp', 'col'), 'row')
- hessian: float32 [16384, 16384], P(('dp', 'col'), 'row')
The draws below stay inside these ranges and needn't reach their ends.
All inputs are finite; a program needn't handle non-finite values. No bound on the sum of `prune_mask` on one device may be relied on, other than what follows from the above.
Results may differ from the reference program's by a relative error of at most 0.001.
Values may be sent and summed in bfloat16 or wider, within the bound.
No kernel may reach another device: no remote copies, remote signals or barrier semaphores. Data moves between devices by JAX's collectives and lax.ppermute only.
A program may use at most 192 MiB of HBM per device.

```python
import math
import jax
import jax.numpy as jnp
from jax import lax

OUT = 8192
REMAIN = 16384
PANEL = 128
KEEP = 8
TOKENS = 2048


def draw_activation(key, part):
    key_scale, key_noise = jax.random.split(key, 2)
    scales = jnp.exp(jax.random.uniform(key_scale, (1, REMAIN), jnp.float32, 0.0, math.log(10.0)))
    noise = jax.random.normal(key_noise, (TOKENS, REMAIN), jnp.float32)
    noise = jnp.clip(noise, -5.0, 5.0)
    return (noise * scales).astype(jnp.bfloat16)


def place_ends(entries, own_key, least, top_value):
    longest = entries.shape.index(max(entries.shape))
    spots = []
    for shift in (0, 1):
        where = [jax.random.randint(jax.random.fold_in(own_key, axis), (), 0, length) for axis, length in enumerate(entries.shape)]
        where[longest] = (where[longest] + shift) % entries.shape[longest]
        spots.append(tuple(where))
    return entries.at[spots[0]].set(least).at[spots[1]].set(top_value)


def shard_levels(own_key, dims, pieces, least, top_value):
    loudness, own = 1.0, jax.random.fold_in(own_key, 6)
    for dim, blocks in pieces:
        heights = jnp.exp(jax.random.uniform(jax.random.fold_in(own, dim), (blocks,), jnp.float32, least / len(pieces), top_value / len(pieces)))
        loudness = loudness * jnp.repeat(heights, dims[dim] // blocks).reshape([-1 if axis == dim else 1 for axis in range(len(dims))])
    return loudness


def gaussian(own_key, extent, spread, reach, cuts=(), kind=jnp.bfloat16):
    drawn = spread * jax.random.normal(own_key, extent, jnp.float32)
    if cuts:
        drawn = drawn * shard_levels(own_key, extent, cuts, -0.22, 0.18)
    return jnp.clip(drawn, -reach, reach).astype(kind)


def setup_inputs(seed: int = 0) -> dict:
    keys = jax.random.split(jax.random.key(seed), 5)
    return {
        "activation": draw_activation(jax.random.fold_in(keys[4], 71), 0),
        "weight": gaussian(keys[1], (OUT, REMAIN), 1.0, 6.0, ((0, 32), (1, 4))),
        "prune_mask": place_ends((jax.random.randint(keys[2], (OUT, PANEL), 0, 2) < 1).astype(jnp.int32), jax.random.fold_in(keys[2], 1), 0, 1),
        "channel_rank": jax.random.permutation(keys[3], PANEL).astype(jnp.int32),
    }


DAMPING = 0.01

def panel_factor(block):
    identity = jnp.eye(block.shape[0], dtype=jnp.float32)
    lower_factor = jnp.linalg.cholesky(block)
    lower_inverse = lax.linalg.triangular_solve(lower_factor, identity, left_side=True, lower=True)
    inverse = jnp.dot(lower_inverse.T, lower_inverse, precision=lax.Precision.HIGHEST)
    return jnp.linalg.cholesky(inverse).T

def panel_sweep(start_cols, keep_weight, factor):
    positions = jnp.arange(start_cols.shape[1])

    def sweep_step(j, carry):
        current, errors = carry
        column = lax.dynamic_index_in_dim(current, j, 1, keepdims=False)
        keep_col = lax.dynamic_index_in_dim(keep_weight, j, 1, keepdims=False)
        factor_row = lax.dynamic_index_in_dim(factor, j, 0, keepdims=False)
        pivot = lax.dynamic_index_in_dim(factor_row, j, 0, keepdims=False)
        error_col = (1.0 - keep_col) * column / pivot
        factor_row = jnp.where(positions > j, factor_row, 0.0)
        current = current - error_col[:, None] * factor_row[None, :]
        errors = lax.dynamic_update_index_in_dim(errors, error_col, j, 1)
        return (current, errors)
    current, errors = lax.fori_loop(0, start_cols.shape[1], sweep_step, (start_cols, jnp.zeros_like(start_cols)))
    return (keep_weight * current, errors)

def reference(activation, weight, prune_mask, channel_rank):
    wide = activation.astype(jnp.float32)
    hessian = jnp.dot(wide.T, wide, precision=lax.Precision.HIGHEST) * (2.0 / TOKENS)
    positions = jnp.arange(REMAIN)
    hessian = hessian.at[positions, positions].add(DAMPING)
    factor = panel_factor(hessian[:PANEL, :PANEL])
    keep_weight = jnp.where((prune_mask == 1) | (channel_rank < KEEP)[None, :], 1.0, 0.0).astype(jnp.float32)
    pruned_panel, errors = panel_sweep(weight[:, :PANEL].astype(jnp.float32), keep_weight, factor)
    correction = jnp.dot(errors, factor, precision=lax.Precision.HIGHEST)
    diagonal = jnp.diagonal(hessian)[PANEL:]
    updated = weight[:, PANEL:].astype(jnp.float32) + jnp.dot(correction, hessian[:PANEL, PANEL:], precision=lax.Precision.HIGHEST) / diagonal[None, :]
    pruned_weight = jnp.concatenate([pruned_panel, updated], axis=1).astype(jnp.bfloat16)
    return (pruned_weight, hessian)
```

```python
import functools

import jax
import jax.numpy as jnp
from jax import lax
from jax.experimental import pallas as pl
from jax.experimental.pallas import tpu as pltpu
from jax.sharding import PartitionSpec as P

PANEL = 128
KEEP = 8
DAMPING = 0.01

NX = 4
NY = 4
NZ = 2
NROW = 4
VMEM_LIMIT = 56 * 1024 * 1024


def x_perm(k):
    return [(i, (i + k) % NX) for i in range(NX)]


def y_perm(k):
    return [(y * NZ + z, ((y + k) % NY) * NZ + z) for y in range(NY) for z in range(NZ)]


Z_PERM = [(y * NZ + z, y * NZ + 1 - z) for y in range(NY) for z in range(NZ)]


def send_x(a, k):
    return lax.ppermute(a, "dp", x_perm(k))


def send_y(a, k):
    return lax.ppermute(a, "col", y_perm(k))


def send_z(a):
    return lax.ppermute(a, "col", Z_PERM)


SHIFTS = (0, -1, 1, 2)


def gather_small(a, send):
    return [a, send(a, 1), send(a, -1), send(a, 2)]


def gather_ring(a, b, send):
    a_left, b_right = send(a, 1), send(b, -1)
    b_left, a_right = send(b, 1), send(a, -1)
    a_far, b_far = send(a_left, 1), send(b_right, -1)
    return [a, a_left, a_right, a_far], [b, b_left, b_right, b_far]


def panel_kernel(ap_ref, wp_ref, mask_ref, rank_ref, corr_ref, panel_ref):
    hess = jnp.zeros((PANEL, PANEL), jnp.float32)
    for k in range(NX):
        blk = ap_ref[k]
        hess += lax.dot_general(blk, blk, (((0,), (0,)), ((), ())), preferred_element_type=jnp.float32)
    tokens = NX * ap_ref.shape[1]
    row = lax.broadcasted_iota(jnp.int32, (PANEL, PANEL), 0)
    col = lax.broadcasted_iota(jnp.int32, (PANEL, PANEL), 1)
    hess = hess * (2.0 / tokens) + jnp.where(row == col, DAMPING, 0.0)
    lane = lax.broadcasted_iota(jnp.int32, (1, PANEL), 1)
    tiles = [hess[8 * t : 8 * t + 8] for t in range(PANEL // 8)]
    ratio = [None] * PANEL
    for j in reversed(range(PANEL)):
        own = tiles[j // 8][j % 8 : j % 8 + 1]
        r = own / own[:, j : j + 1]
        ratio[j] = jnp.where(lane < j, r, 0.0)
        for t in range((j + 7) // 8):
            tiles[t] = tiles[t] - tiles[t][:, j : j + 1] * r
    ratio_tiles = [jnp.concatenate(ratio[8 * t : 8 * t + 8], axis=0) for t in range(PANEL // 8)]

    keep = jnp.where((mask_ref[...] == 1) | (rank_ref[...] < KEEP), 1.0, 0.0)
    keep_t = keep.T
    w_t = wp_ref[...].astype(jnp.float32).T
    rows = w_t.shape[1]
    acc = [jnp.zeros((8, rows), jnp.float32) for _ in range(PANEL // 8)]
    corr = [None] * PANEL
    for j in range(PANEL):
        c = jnp.where(keep_t[j : j + 1] > 0.5, -acc[j // 8][j % 8 : j % 8 + 1], w_t[j : j + 1])
        corr[j] = c
        for t in range((j + 1) // 8, PANEL // 8):
            acc[t] = acc[t] + ratio_tiles[t][:, j : j + 1] * c
    corr_t = jnp.concatenate(corr, axis=0)
    corr_ref[...] = corr_t.T
    panel_ref[...] = jnp.where(keep_t > 0.5, w_t - corr_t, 0.0).T.astype(panel_ref.dtype)


def panel_step(ap, wp, mask, rank):
    rows = wp.shape[0]
    return pl.pallas_call(
        panel_kernel,
        out_shape=(
            jax.ShapeDtypeStruct((rows, PANEL), jnp.float32),
            jax.ShapeDtypeStruct((rows, PANEL), jnp.bfloat16),
        ),
        compiler_params=pltpu.CompilerParams(vmem_limit_bytes=VMEM_LIMIT),
        name="panel_sweep",
    )(ap, wp, mask, rank.reshape(1, PANEL))


def columns_kernel(entry_axis, tok, scale, info, lhs_ref, corr_ref, panel_ref, w_ref, *rest):
    pieces = rest[:NX] if entry_axis else rest[:1]
    out_ref, hess_ref = rest[-2], rest[-1]
    rows = hess_ref.shape[0]
    step = pl.program_id(0)
    acc = None
    diag = None
    for k in range(NX):
        piece = pieces[k][0] if entry_axis else pieces[0][k]
        part = jnp.dot(lhs_ref[:, k * tok : (k + 1) * tok], piece, preferred_element_type=jnp.float32)
        acc = part if acc is None else acc + part
        wide = piece.astype(jnp.float32)
        square = jnp.sum(wide * wide, axis=0, keepdims=True)
        diag = square if diag is None else diag + square
    acc = acc * scale
    diag = diag * scale + DAMPING
    col0 = info[0] + info[2 + step] * hess_ref.shape[1]
    hess = acc[:rows]
    row = lax.broadcasted_iota(jnp.int32, hess.shape, 0)
    col = lax.broadcasted_iota(jnp.int32, hess.shape, 1)
    hess_ref[...] = hess + jnp.where(row - col == col0 - info[1], DAMPING, 0.0)
    change = jnp.dot(
        corr_ref[...], acc[rows:], precision=lax.Precision.HIGHEST, preferred_element_type=jnp.float32
    )
    out_ref[...] = (w_ref[...].astype(jnp.float32) + change / diag).astype(out_ref.dtype)

    @pl.when(col0 == 0)
    def _():
        out_ref[:, :PANEL] = panel_ref[...]


def columns_step(info, lhs, corr, panel, weight, pieces, entry_axis, out, hess):
    entries = pieces[0].shape[0] if entry_axis else 1
    tok, width = pieces[0].shape[1:]
    out_rows, chans = weight.shape
    rows = lhs.shape[0] - PANEL
    fixed = lambda i, info: (0, 0)
    at_block = lambda i, info: (0, info[2 + i])
    in_specs = [
        pl.BlockSpec(lhs.shape, fixed),
        pl.BlockSpec(corr.shape, fixed),
        pl.BlockSpec(panel.shape, fixed),
        pl.BlockSpec((out_rows, width), at_block),
    ]
    if entry_axis:
        in_specs += [pl.BlockSpec((1, tok, width), lambda i, info: (i, 0, 0))] * NX
    else:
        in_specs += [pl.BlockSpec((NX, tok, width), lambda i, info: (0, 0, 0))]
    operands = [lhs, corr, panel, weight, *pieces]
    aliases = {}
    if out is not None:
        in_specs += [pl.BlockSpec(memory_space=pl.ANY)] * 2
        operands += [out, hess]
        aliases = {len(operands) - 1: 0, len(operands): 1}
    body = functools.partial(columns_kernel, entry_axis, tok, 2.0 / (NX * tok))
    return pl.pallas_call(
        body,
        grid_spec=pltpu.PrefetchScalarGridSpec(
            num_scalar_prefetch=1,
            grid=(entries,),
            in_specs=in_specs,
            out_specs=(
                pl.BlockSpec((out_rows, width), at_block),
                pl.BlockSpec((rows, width), at_block),
            ),
        ),
        out_shape=(
            jax.ShapeDtypeStruct((out_rows, chans), weight.dtype),
            jax.ShapeDtypeStruct((rows, chans), jnp.float32),
        ),
        input_output_aliases=aliases,
        compiler_params=pltpu.CompilerParams(vmem_limit_bytes=VMEM_LIMIT),
        name="columns",
    )(info, *operands)


def body(activation, weight, prune_mask, channel_rank):
    tok, block = activation.shape
    chans = weight.shape[1]
    d, r, c = lax.axis_index("dp"), lax.axis_index("row"), lax.axis_index("col")
    y, z = c // NZ, c % NZ
    ncol = NY * NZ

    ap = activation[:, :PANEL]
    ap = jnp.where((r == 0) & (c == 0), ap, jnp.zeros_like(ap))
    got = [lax.ppermute(ap, ("row", "col"), [(0, k)]) for k in range(1, ncol)]
    ap = functools.reduce(jnp.add, got, ap)
    got = [lax.ppermute(ap, ("row", "col"), [(i, k * ncol + i) for i in range(ncol)]) for k in range(1, NROW)]
    ap = functools.reduce(jnp.add, got, ap)
    ap = jnp.stack(gather_small(ap, send_x))
    wp = jnp.where(r == 0, weight[:, :PANEL], jnp.zeros_like(weight[:, :PANEL]))
    wp = functools.reduce(jnp.add, [lax.ppermute(wp, "row", [(0, k)]) for k in range(1, NROW)], wp)
    corr, panel = panel_step(ap, wp, prune_mask, channel_rank)

    swap = [(i * NROW + j, j * NROW + i) for i in range(NX) for j in range(NROW)]
    own = lax.ppermute(activation, ("dp", "row"), swap)
    core = lax.ppermute(own, "row", [(i, i ^ 1) for i in range(NROW)])
    pair = [own, core]
    pair += [lax.ppermute(p, "row", [(i, i ^ 2) for i in range(NROW)]) for p in (own, core)]
    stacked = jnp.stack(pair)
    rows = [lax.dynamic_index_in_dim(stacked, ((d + s) % NX) ^ r, 0, keepdims=False) for s in SHIFTS]
    lhs = jnp.concatenate(
        [jnp.concatenate(rows, axis=0), ap.reshape(NX * tok, PANEL)], axis=1
    ).T

    half = block // 2
    first = activation[:, :half]
    near = jnp.stack(gather_small(first, send_y))
    first_a, first_b = gather_ring(near, send_z(near), send_x)
    second = activation[:, half:]
    second_z = send_z(second)
    second_a, second_b = gather_ring(
        jnp.stack(gather_small(second, send_x)), jnp.stack(gather_small(second_z, send_x)), send_y
    )

    base = jnp.stack([r * chans, (d * ncol + c) * block])

    def info(cols, part):
        return jnp.concatenate([base, jnp.stack([k * 2 + part for k in cols])]).astype(jnp.int32)

    def cblock(dy, dz):
        return ((y + dy) % NY) * NZ + (z + dz) % NZ

    out = hess = None
    for i in range(len(SHIFTS)):
        for dz, arrays in ((0, second_a), (1, second_b)):
            cols = info([cblock(SHIFTS[i], dz)], 1)
            out, hess = columns_step(cols, lhs, corr, panel, weight, [arrays[i]], False, out, hess)
    for dz, arrays in ((0, first_a), (1, first_b)):
        cols = info([cblock(s, dz) for s in SHIFTS], 0)
        out, hess = columns_step(cols, lhs, corr, panel, weight, arrays, True, out, hess)
    return (out, hess)


def solution(mesh):
    return jax.shard_map(
        body,
        mesh=mesh,
        in_specs=(P("dp", ("row", "col")), P(("dp", "col"), "row"), P(("dp", "col"), None), P()),
        out_specs=(P(("dp", "col"), "row"), P(("dp", "col"), "row")),
        check_vma=False,
    )
```

```python
import functools

import jax
import jax.numpy as jnp
from jax import lax
from jax.experimental import pallas as pl
from jax.experimental.pallas import tpu as pltpu
from jax.sharding import PartitionSpec as P

PANEL = 128
KEEP = 8
DAMPING = 0.01

NX = 4
NY = 4
NZ = 2
NROW = 4
VMEM_LIMIT = 56 * 1024 * 1024


def x_perm(k):
    return [(i, (i + k) % NX) for i in range(NX)]


def y_perm(k):
    return [(y * NZ + z, ((y + k) % NY) * NZ + z) for y in range(NY) for z in range(NZ)]


Z_PERM = [(y * NZ + z, y * NZ + 1 - z) for y in range(NY) for z in range(NZ)]


def send_x(a, k):
    return lax.ppermute(a, "dp", x_perm(k))


def send_y(a, k):
    return lax.ppermute(a, "col", y_perm(k))


def send_z(a):
    return lax.ppermute(a, "col", Z_PERM)


SHIFTS = (0, -1, 1, 2)


def ring_near(a, send):
    return send(a, 1), send(a, -1)


def ring_out(a, b, send):
    return send(a, 1), send(b, -1)


def ring_in(a, b, send):
    return send(b, 1), send(a, -1)


def ring_far(left, right, send):
    mid = left.shape[0] // 2
    return send(left[:mid], 1), send(right[mid:], -1)


def panel_kernel(ap_ref, wp_ref, mask_ref, rank_ref, corr_ref, panel_ref):
    hess = jnp.zeros((PANEL, PANEL), jnp.float32)
    for k in range(NX):
        blk = ap_ref[k]
        hess += lax.dot_general(blk, blk, (((0,), (0,)), ((), ())), preferred_element_type=jnp.float32)
    tokens = NX * ap_ref.shape[1]
    row = lax.broadcasted_iota(jnp.int32, (PANEL, PANEL), 0)
    col = lax.broadcasted_iota(jnp.int32, (PANEL, PANEL), 1)
    hess = hess * (2.0 / tokens) + jnp.where(row == col, DAMPING, 0.0)
    lane = lax.broadcasted_iota(jnp.int32, (1, PANEL), 1)
    tiles = [hess[8 * t : 8 * t + 8] for t in range(PANEL // 8)]
    ratio = [None] * PANEL
    for j in reversed(range(PANEL)):
        own = tiles[j // 8][j % 8 : j % 8 + 1]
        r = own / own[:, j : j + 1]
        ratio[j] = jnp.where(lane < j, r, 0.0)
        for t in range((j + 7) // 8):
            tiles[t] = tiles[t] - tiles[t][:, j : j + 1] * r
    ratio_tiles = [jnp.concatenate(ratio[8 * t : 8 * t + 8], axis=0) for t in range(PANEL // 8)]

    keep = jnp.where((mask_ref[...] == 1) | (rank_ref[...] < KEEP), 1.0, 0.0)
    keep_t = keep.T
    w_t = wp_ref[...].astype(jnp.float32).T
    rows = w_t.shape[1]
    acc = [jnp.zeros((8, rows), jnp.float32) for _ in range(PANEL // 8)]
    corr = [None] * PANEL
    for j in range(PANEL):
        c = jnp.where(keep_t[j : j + 1] > 0.5, -acc[j // 8][j % 8 : j % 8 + 1], w_t[j : j + 1])
        corr[j] = c
        for t in range((j + 1) // 8, PANEL // 8):
            acc[t] = acc[t] + ratio_tiles[t][:, j : j + 1] * c
    corr_t = jnp.concatenate(corr, axis=0)
    corr_ref[...] = corr_t.T
    panel_ref[...] = jnp.where(keep_t > 0.5, w_t - corr_t, 0.0).T.astype(panel_ref.dtype)


def panel_step(ap, wp, mask, rank):
    rows = wp.shape[0]
    return pl.pallas_call(
        panel_kernel,
        out_shape=(
            jax.ShapeDtypeStruct((rows, PANEL), jnp.float32),
            jax.ShapeDtypeStruct((rows, PANEL), jnp.bfloat16),
        ),
        compiler_params=pltpu.CompilerParams(vmem_limit_bytes=VMEM_LIMIT),
        cost_estimate=pl.CostEstimate(flops=1 << 33, transcendentals=0, bytes_accessed=1 << 25),
        name="panel_sweep",
    )(ap, wp, mask, rank.reshape(1, PANEL))


def lhs_kernel(block, info, own_ref, own_z_ref, core_ref, ap_ref, lhs_ref):
    tok = own_ref.shape[0]
    for m, piece in enumerate((own_ref, core_ref.at[0], own_z_ref, core_ref.at[1])):
        lhs_ref[:block, pl.ds(pl.multiple_of(info[m] * tok, tok), tok)] = piece[...].T
    for k in range(NX):
        lhs_ref[block:, k * tok : (k + 1) * tok] = ap_ref[k].T


def lhs_step(slots, own, own_z, core, ap):
    tok, block = own.shape
    shape = (block + PANEL, NX * tok)
    whole = pl.BlockSpec(memory_space=pltpu.VMEM)
    return pl.pallas_call(
        functools.partial(lhs_kernel, block),
        out_shape=jax.ShapeDtypeStruct(shape, own.dtype),
        in_specs=[pl.BlockSpec(memory_space=pltpu.SMEM)] + [whole] * 4,
        out_specs=whole,
        compiler_params=pltpu.CompilerParams(vmem_limit_bytes=VMEM_LIMIT),
        cost_estimate=pl.CostEstimate(flops=1 << 31, transcendentals=0, bytes_accessed=1 << 23),
        name="lhs",
    )(slots, own, own_z, core, ap)


def columns_kernel(pairs, tok, width, n_pieces, has_in, has_out, info, lhs_ref, corr_ref, panel_ref, w_hbm, *rest):
    pieces = rest[:n_pieces]
    part_in = rest[n_pieces] if has_in else None
    x_buf, w_buf, out_buf, hess_buf, part_buf, in_sem, out_sem = rest[-7:]
    outs = rest[-10:-7] if has_out else (*rest[-9:-7], None)
    out_hbm, hess_hbm, part_out = outs
    rows = hess_buf.shape[1]
    all_rows = lhs_ref.shape[0]
    scale = 2.0 / (NX * tok)

    def column(p, h):
        return pl.multiple_of(info[2 + 2 * p + h] * width, width)

    def loads(p):
        slot = p % 2
        low, high, places, begin, leave = pairs[p]
        copies = []
        for h in range(2):
            lanes = pl.ds(h * width, width)
            for k in range(high - low):
                which, lead = places[h][k]
                copies.append((pieces[which].at[lead], x_buf.at[slot, pl.ds(k * tok, tok), lanes]))
            if leave is None:
                copies.append((w_hbm.at[:, pl.ds(column(p, h), width)], w_buf.at[slot, :, lanes]))
        if begin is not None:
            copies.append((part_in.at[begin], part_buf.at[slot]))
        return [pltpu.make_async_copy(a, b, in_sem.at[slot, n]) for n, (a, b) in enumerate(copies)]

    def stores(p):
        slot = p % 2
        leave = pairs[p][4]
        copies = []
        if leave is not None:
            copies.append((part_buf.at[slot], part_out.at[leave]))
        else:
            for h in range(2):
                lanes = pl.ds(h * width, width)
                copies.append((hess_buf.at[slot, :, lanes], hess_hbm.at[:, pl.ds(column(p, h), width)]))
                copies.append((out_buf.at[slot, :, lanes], out_hbm.at[:, pl.ds(column(p, h), width)]))
        return [pltpu.make_async_copy(a, b, out_sem.at[slot, n]) for n, (a, b) in enumerate(copies)]

    for copy in loads(0):
        copy.start()
    for p in range(len(pairs)):
        slot = p % 2
        low, high, _, begin, leave = pairs[p]
        if p + 1 < len(pairs):
            for copy in loads(p + 1):
                copy.start()
        for copy in loads(p):
            copy.wait()
        if p >= 2:
            for copy in stores(p - 2):
                copy.wait()
        x = x_buf[slot, : (high - low) * tok]
        acc = jnp.dot(lhs_ref[:, low * tok : high * tok], x, preferred_element_type=jnp.float32)
        wide = x.astype(jnp.float32)
        diag = jnp.sum(wide * wide, axis=0, keepdims=True)
        if begin is not None:
            acc = acc + part_buf[slot, :all_rows]
            diag = diag + part_buf[slot, all_rows : all_rows + 1]
        if leave is not None:
            part_buf[slot, :all_rows] = acc
            part_buf[slot, all_rows:] = jnp.broadcast_to(diag, (8, 2 * width))
        else:
            acc = acc * scale
            diag = diag * scale + DAMPING
            change = jnp.dot(
                corr_ref[...],
                acc[rows:] / diag,
                precision=lax.Precision.HIGHEST,
                preferred_element_type=jnp.float32,
            )
            out_buf[slot] = (w_buf[slot].astype(jnp.float32) + change).astype(out_buf.dtype)
            row = lax.broadcasted_iota(jnp.int32, (rows, width), 0)
            col = lax.broadcasted_iota(jnp.int32, (rows, width), 1)
            for h in range(2):
                lanes = slice(h * width, (h + 1) * width)
                col0 = info[0] + column(p, h)
                hess_buf[slot, :, lanes] = acc[:rows, lanes] + jnp.where(row - col == col0 - info[1], DAMPING, 0.0)

                @pl.when(col0 == 0)
                def _():
                    out_buf[slot, :, h * width : h * width + PANEL] = panel_ref[...]

        for copy in stores(p):
            copy.start()
    for p in range(max(0, len(pairs) - 2), len(pairs)):
        for copy in stores(p):
            copy.wait()


def columns_step(base, lhs, corr, panel, weight, pieces, entries, low, high, begin, leave, parts, out, hess):
    tok, width = pieces[0].shape[1:]
    out_rows, chans = weight.shape
    rows = lhs.shape[0] - PANEL
    info = jnp.concatenate([base, jnp.stack([place for place, _ in entries])]).astype(jnp.int32)
    pairs = [
        (low[i], high[i], (entries[2 * i][1], entries[2 * i + 1][1]), begin[i], leave[i])
        for i in range(len(entries) // 2)
    ]
    n_out = sum(a is not None for a in leave)
    fixed = lambda i, info: (0, 0)
    anywhere = pl.BlockSpec(memory_space=pltpu.HBM)
    operands = [lhs, corr, panel, weight, *pieces]
    if parts is not None:
        operands.append(parts)
    in_specs = [pl.BlockSpec(a.shape, fixed) for a in (lhs, corr, panel)] + [anywhere] * (len(operands) - 3)
    aliases = {}
    if out is not None:
        in_specs += [anywhere] * 2
        operands += [out, hess]
        aliases = {len(operands) - 1: 0, len(operands): 1}
    part = (lhs.shape[0] + 8, 2 * width)
    out_shape = [
        jax.ShapeDtypeStruct((out_rows, chans), weight.dtype),
        jax.ShapeDtypeStruct((rows, chans), jnp.float32),
    ]
    if n_out:
        out_shape.append(jax.ShapeDtypeStruct((n_out, *part), jnp.float32))
    body = functools.partial(columns_kernel, pairs, tok, width, len(pieces), parts is not None, n_out > 0)
    total = len(entries) * width
    return pl.pallas_call(
        body,
        grid_spec=pltpu.PrefetchScalarGridSpec(
            num_scalar_prefetch=1,
            grid=(1,),
            in_specs=in_specs,
            out_specs=[anywhere] * len(out_shape),
            scratch_shapes=[
                pltpu.VMEM((2, NX * tok, 2 * width), jnp.bfloat16),
                pltpu.VMEM((2, out_rows, 2 * width), weight.dtype),
                pltpu.VMEM((2, out_rows, 2 * width), weight.dtype),
                pltpu.VMEM((2, rows, 2 * width), jnp.float32),
                pltpu.VMEM((2, *part), jnp.float32),
                pltpu.SemaphoreType.DMA((2, 2 * NX + 3)),
                pltpu.SemaphoreType.DMA((2, 4)),
            ],
        ),
        out_shape=out_shape,
        input_output_aliases=aliases,
        compiler_params=pltpu.CompilerParams(vmem_limit_bytes=VMEM_LIMIT),
        cost_estimate=pl.CostEstimate(
            flops=2 * total * NX * tok * lhs.shape[0],
            transcendentals=0,
            bytes_accessed=total * (NX * tok * 2 + rows * 4 + out_rows * 4) + lhs.size * 2,
        ),
        name="columns",
    )(info, *operands)


def body(activation, weight, prune_mask, channel_rank):
    tok, block = activation.shape
    chans = weight.shape[1]
    d, r, c = lax.axis_index("dp"), lax.axis_index("row"), lax.axis_index("col")
    y, z = c // NZ, c % NZ
    ncol = NY * NZ
    half = block // 2

    other = send_z(activation)

    everywhere = ("dp", "row", "col")
    per_x = NROW * ncol
    ap = jnp.where((r == 0) & (c == 0), activation[:, :PANEL], jnp.zeros((tok, PANEL), activation.dtype))
    ap = functools.reduce(
        jnp.add, [lax.ppermute(ap, ("row", "col"), [(0, k * NZ)]) for k in range(1, NY)], ap
    )
    ap, other, activation = lax.optimization_barrier((ap, other, activation))
    swap = [(i * NROW + j, j * NROW + i) for i in range(NX) for j in range(NROW)]
    own = lax.ppermute(activation, ("dp", "row"), swap)
    ap = jnp.concatenate(
        [ap]
        + [
            lax.ppermute(ap, everywhere, [(a * per_x + k * NZ, b * per_x + k * NZ) for a, b in x_perm(s) for k in range(NY)])
            for s in (1, -1, 2)
        ]
    )
    other, ap, activation = lax.optimization_barrier((other, ap, activation))

    first = jnp.stack([activation[:, :half], other[:, :half]])
    second = jnp.stack([activation[:, half:], other[:, half:]])
    first_left, first_right = ring_near(first, send_y)
    second_left, second_right = ring_near(second, send_x)
    ap = ap + lax.ppermute(ap, ("row", "col"), [(i, i + 1) for i in range(0, ncol, NZ)])
    first_left, first_right, second_left, second_right, ap = lax.optimization_barrier(
        (first_left, first_right, second_left, second_right, ap)
    )
    first_far = ring_far(first_left, first_right, send_y)
    second_far = ring_far(second_left, second_right, send_x)
    wp = jnp.where(r == 0, weight[:, :PANEL], jnp.zeros_like(weight[:, :PANEL]))
    both = jnp.concatenate([ap, wp])
    both = both + lax.ppermute(both, "row", [(0, 1)])
    both = both + lax.ppermute(both, "row", [(0, 2), (1, 3)])
    first = (jnp.concatenate([first, first_left]), jnp.concatenate([first_right, *first_far]))
    second = (jnp.concatenate([second, second_left]), jnp.concatenate([second_right, *second_far]))
    first, second, both, own = lax.optimization_barrier((first, second, both, own))

    first_out, second_out = ring_out(*first, send_x), ring_out(*second, send_y)
    ap, wp = both[: NX * tok].reshape(NX, tok, PANEL), both[NX * tok :]
    corr, panel = panel_step(ap, wp, prune_mask, channel_rank)
    own_z = lax.ppermute(own, "row", [(i, i ^ 2) for i in range(NROW)])
    first, second, first_out, second_out, corr, own_z = lax.optimization_barrier(
        (first, second, first_out, second_out, corr, own_z)
    )
    first_in, second_in = ring_in(*first, send_x), ring_in(*second, send_y)
    core = lax.ppermute(jnp.stack([own, own_z]), "row", [(i, i ^ 1) for i in range(NROW)])
    order = jnp.array([0, 2, 3, 1], jnp.int32)
    lhs = lhs_step(order[((r ^ jnp.arange(NROW)) - d) % NX], own, own_z, core, ap)
    first_out, second_out, first_in, second_in, lhs = lax.optimization_barrier(
        (first_out, second_out, first_in, second_in, lhs)
    )
    first_far, second_far = ring_out(*first_out, send_x), ring_out(*second_out, send_y)

    base = jnp.stack([r * chans, (d * ncol + c) * block])
    step = functools.partial(columns_step, base, lhs, corr, panel, weight)

    def place(dy, dz, part):
        return (((y + dy) % NY) * NZ + (z + dz) % NZ) * 2 + part

    def second_entries(shifts):
        return [
            (place(s, dz, 1), [(2 * i + k // 2, (k % 2) * NZ + dz) for k in range(NX)])
            for i, s in enumerate(shifts)
            for dz in range(NZ)
        ]

    def first_entries(skip, ks):
        return [
            (place(s, dz, 0), [(skip + 2 * k + i // 2, (i % 2) * NZ + dz) for k in ks])
            for i, s in enumerate(SHIFTS)
            for dz in range(NZ)
        ]

    far = NX - 1
    pieces = [*second, second_out[0], second_in[0], second_in[1], second_out[1]]
    skip = len(pieces)
    pieces += [*first, first_out[0], first_in[0], first_in[1], first_out[1]]
    entries = second_entries(SHIFTS[:far]) + first_entries(skip, range(far))
    none, slots = [None] * NX, list(range(NX))
    out, hess, parts = step(
        pieces, entries, [0] * 7, [NX] * 3 + [far] * 4, [None] * 7, none[:3] + slots, None, None, None
    )
    entries = second_entries(SHIFTS[far:])
    entries += [(place, [(2 + which, lead)]) for place, ((which, lead),) in first_entries(0, [0])]
    out, hess = step(
        [*second_far, *first_far], entries, [0] + [far] * 4, [NX] * 5, [None] + slots, [None] * 5, parts, out, hess
    )
    return (out, hess)


def solution(mesh):
    return jax.shard_map(
        body,
        mesh=mesh,
        in_specs=(P("dp", ("row", "col")), P(("dp", "col"), "row"), P(("dp", "col"), None), P()),
        out_specs=(P(("dp", "col"), "row"), P(("dp", "col"), "row")),
        check_vma=False,
    )
```

```python
import functools

import jax
import jax.numpy as jnp
from jax import lax
from jax.experimental import pallas as pl
from jax.experimental.pallas import tpu as pltpu
from jax.sharding import PartitionSpec as P

PANEL = 128
KEEP = 8
DAMPING = 0.01

NX = 4
NY = 4
NZ = 2
NROW = 4
VMEM_LIMIT = 56 * 1024 * 1024


def x_perm(k):
    return [(i, (i + k) % NX) for i in range(NX)]


def y_perm(k):
    return [(y * NZ + z, ((y + k) % NY) * NZ + z) for y in range(NY) for z in range(NZ)]


Z_PERM = [(y * NZ + z, y * NZ + 1 - z) for y in range(NY) for z in range(NZ)]


def send_x(a, k):
    return lax.ppermute(a, "dp", x_perm(k))


def send_y(a, k):
    return lax.ppermute(a, "col", y_perm(k))


def send_z(a):
    return lax.ppermute(a, "col", Z_PERM)


SHIFTS = (0, -1, 1, 2)


def ring_near(a, send):
    return send(a, 1), send(a, -1)


def ring_out(a, b, send):
    return send(a, 1), send(b, -1)


def ring_in(a, b, send):
    return send(b, 1), send(a, -1)


def ring_far(left, right, send):
    mid = left.shape[0] // 2
    return send(left[:mid], 1), send(right[mid:], -1)


def panel_kernel(ap_ref, wp_ref, mask_ref, rank_ref, corr_ref, panel_ref):
    hess = jnp.zeros((PANEL, PANEL), jnp.float32)
    for k in range(NX):
        blk = ap_ref[k]
        hess += lax.dot_general(blk, blk, (((0,), (0,)), ((), ())), preferred_element_type=jnp.float32)
    tokens = NX * ap_ref.shape[1]
    row = lax.broadcasted_iota(jnp.int32, (PANEL, PANEL), 0)
    col = lax.broadcasted_iota(jnp.int32, (PANEL, PANEL), 1)
    hess = hess * (2.0 / tokens) + jnp.where(row == col, DAMPING, 0.0)
    lane = lax.broadcasted_iota(jnp.int32, (1, PANEL), 1)
    tiles = [hess[8 * t : 8 * t + 8] for t in range(PANEL // 8)]
    ratio = [None] * PANEL
    for j in reversed(range(PANEL)):
        own = tiles[j // 8][j % 8 : j % 8 + 1]
        r = own / own[:, j : j + 1]
        ratio[j] = jnp.where(lane < j, r, 0.0)
        for t in range((j + 7) // 8):
            tiles[t] = tiles[t] - tiles[t][:, j : j + 1] * r
    ratio_tiles = [jnp.concatenate(ratio[8 * t : 8 * t + 8], axis=0) for t in range(PANEL // 8)]

    keep = jnp.where((mask_ref[...] == 1) | (rank_ref[...] < KEEP), 1.0, 0.0)
    keep_t = keep.T
    w_t = wp_ref[...].astype(jnp.float32).T
    rows = w_t.shape[1]
    acc = [jnp.zeros((8, rows), jnp.float32) for _ in range(PANEL // 8)]
    corr = [None] * PANEL
    for j in range(PANEL):
        c = jnp.where(keep_t[j : j + 1] > 0.5, -acc[j // 8][j % 8 : j % 8 + 1], w_t[j : j + 1])
        corr[j] = c
        for t in range((j + 1) // 8, PANEL // 8):
            acc[t] = acc[t] + ratio_tiles[t][:, j : j + 1] * c
    corr_t = jnp.concatenate(corr, axis=0)
    corr_ref[...] = corr_t.T
    panel_ref[...] = jnp.where(keep_t > 0.5, w_t - corr_t, 0.0).T.astype(panel_ref.dtype)


def panel_step(ap, wp, mask, rank):
    rows = wp.shape[0]
    return pl.pallas_call(
        panel_kernel,
        out_shape=(
            jax.ShapeDtypeStruct((rows, PANEL), jnp.float32),
            jax.ShapeDtypeStruct((rows, PANEL), jnp.bfloat16),
        ),
        compiler_params=pltpu.CompilerParams(vmem_limit_bytes=VMEM_LIMIT),
        cost_estimate=pl.CostEstimate(flops=1 << 33, transcendentals=0, bytes_accessed=1 << 25),
        name="panel_sweep",
    )(ap, wp, mask, rank.reshape(1, PANEL))


def lhs_kernel(block, info, own_ref, own_z_ref, core_ref, ap_ref, lhs_ref):
    tok = own_ref.shape[0]
    for m, piece in enumerate((own_ref, core_ref.at[0], own_z_ref, core_ref.at[1])):
        lhs_ref[:block, pl.ds(pl.multiple_of(info[m] * tok, tok), tok)] = piece[...].T
    for k in range(NX):
        lhs_ref[block:, k * tok : (k + 1) * tok] = ap_ref[k].T


def lhs_step(slots, own, own_z, core, ap):
    tok, block = own.shape
    shape = (block + PANEL, NX * tok)
    whole = pl.BlockSpec(memory_space=pltpu.VMEM)
    return pl.pallas_call(
        functools.partial(lhs_kernel, block),
        out_shape=jax.ShapeDtypeStruct(shape, own.dtype),
        in_specs=[pl.BlockSpec(memory_space=pltpu.SMEM)] + [whole] * 4,
        out_specs=whole,
        compiler_params=pltpu.CompilerParams(vmem_limit_bytes=VMEM_LIMIT),
        cost_estimate=pl.CostEstimate(flops=1 << 31, transcendentals=0, bytes_accessed=1 << 23),
        name="lhs",
    )(slots, own, own_z, core, ap)


def columns_kernel(pairs, tok, width, n_pieces, has_in, has_out, info, lhs_ref, corr_ref, panel_ref, w_hbm, *rest):
    pieces = rest[:n_pieces]
    part_in = rest[n_pieces] if has_in else None
    x_buf, w_buf, out_buf, hess_buf, part_buf, in_sem, out_sem = rest[-7:]
    outs = rest[-10:-7] if has_out else (*rest[-9:-7], None)
    out_hbm, hess_hbm, part_out = outs
    rows = hess_buf.shape[1]
    all_rows = lhs_ref.shape[0]
    scale = 2.0 / (NX * tok)

    def column(p, h):
        return pl.multiple_of(info[2 + 2 * p + h] * width, width)

    def loads(p):
        slot = p % 2
        low, high, places, begin, leave = pairs[p]
        copies = []
        for h in range(2):
            lanes = pl.ds(h * width, width)
            for k in range(high - low):
                which, lead = places[h][k]
                copies.append((pieces[which].at[lead], x_buf.at[slot, pl.ds(k * tok, tok), lanes]))
            if leave is None:
                copies.append((w_hbm.at[:, pl.ds(column(p, h), width)], w_buf.at[slot, :, lanes]))
        if begin is not None:
            copies.append((part_in.at[begin], part_buf.at[slot]))
        return [pltpu.make_async_copy(a, b, in_sem.at[slot, n]) for n, (a, b) in enumerate(copies)]

    def stores(p):
        slot = p % 2
        leave = pairs[p][4]
        copies = []
        if leave is not None:
            copies.append((part_buf.at[slot], part_out.at[leave]))
        else:
            for h in range(2):
                lanes = pl.ds(h * width, width)
                copies.append((hess_buf.at[slot, :, lanes], hess_hbm.at[:, pl.ds(column(p, h), width)]))
                copies.append((out_buf.at[slot, :, lanes], out_hbm.at[:, pl.ds(column(p, h), width)]))
        return [pltpu.make_async_copy(a, b, out_sem.at[slot, n]) for n, (a, b) in enumerate(copies)]

    for copy in loads(0):
        copy.start()
    for p in range(len(pairs)):
        slot = p % 2
        low, high, _, begin, leave = pairs[p]
        if p + 1 < len(pairs):
            for copy in loads(p + 1):
                copy.start()
        for copy in loads(p):
            copy.wait()
        if p >= 2:
            for copy in stores(p - 2):
                copy.wait()
        x = x_buf[slot, : (high - low) * tok]
        acc = jnp.dot(lhs_ref[:, low * tok : high * tok], x, preferred_element_type=jnp.float32)
        wide = x.astype(jnp.float32)
        diag = jnp.sum(wide * wide, axis=0, keepdims=True)
        if begin is not None:
            acc = acc + part_buf[slot, :all_rows]
            diag = diag + part_buf[slot, all_rows : all_rows + 1]
        if leave is not None:
            part_buf[slot, :all_rows] = acc
            part_buf[slot, all_rows:] = jnp.broadcast_to(diag, (8, 2 * width))
        else:
            acc = acc * scale
            diag = diag * scale + DAMPING
            change = jnp.dot(
                corr_ref[...],
                acc[rows:] / diag,
                precision=lax.Precision.HIGHEST,
                preferred_element_type=jnp.float32,
            )
            out_buf[slot] = (w_buf[slot].astype(jnp.float32) + change).astype(out_buf.dtype)
            hess_buf[slot] = acc[:rows]
            for h in range(2):
                lanes = slice(h * width, (h + 1) * width)
                col0 = info[0] + column(p, h)
                ahead = col0 - info[1]

                @pl.when((ahead > -width) & (ahead < rows))
                def _():
                    row = lax.broadcasted_iota(jnp.int32, (rows, width), 0)
                    col = lax.broadcasted_iota(jnp.int32, (rows, width), 1)
                    hess_buf[slot, :, lanes] = hess_buf[slot, :, lanes] + jnp.where(row - col == ahead, DAMPING, 0.0)

                @pl.when(col0 == 0)
                def _():
                    out_buf[slot, :, h * width : h * width + PANEL] = panel_ref[...]

        for copy in stores(p):
            copy.start()
    for p in range(max(0, len(pairs) - 2), len(pairs)):
        for copy in stores(p):
            copy.wait()


def columns_step(base, lhs, corr, panel, weight, pieces, entries, low, high, begin, leave, parts, out, hess):
    tok, width = pieces[0].shape[1:]
    out_rows, chans = weight.shape
    rows = lhs.shape[0] - PANEL
    info = jnp.concatenate([base, jnp.stack([place for place, _ in entries])]).astype(jnp.int32)
    pairs = [
        (low[i], high[i], (entries[2 * i][1], entries[2 * i + 1][1]), begin[i], leave[i])
        for i in range(len(entries) // 2)
    ]
    n_out = sum(a is not None for a in leave)
    fixed = lambda i, info: (0, 0)
    anywhere = pl.BlockSpec(memory_space=pltpu.HBM)
    operands = [lhs, corr, panel, weight, *pieces]
    if parts is not None:
        operands.append(parts)
    in_specs = [pl.BlockSpec(a.shape, fixed) for a in (lhs, corr, panel)] + [anywhere] * (len(operands) - 3)
    aliases = {}
    if out is not None:
        in_specs += [anywhere] * 2
        operands += [out, hess]
        aliases = {len(operands) - 1: 0, len(operands): 1}
    part = (lhs.shape[0] + 8, 2 * width)
    out_shape = [
        jax.ShapeDtypeStruct((out_rows, chans), weight.dtype),
        jax.ShapeDtypeStruct((rows, chans), jnp.float32),
    ]
    if n_out:
        out_shape.append(jax.ShapeDtypeStruct((n_out, *part), jnp.float32))
    body = functools.partial(columns_kernel, pairs, tok, width, len(pieces), parts is not None, n_out > 0)
    total = len(entries) * width
    return pl.pallas_call(
        body,
        grid_spec=pltpu.PrefetchScalarGridSpec(
            num_scalar_prefetch=1,
            grid=(1,),
            in_specs=in_specs,
            out_specs=[anywhere] * len(out_shape),
            scratch_shapes=[
                pltpu.VMEM((2, NX * tok, 2 * width), jnp.bfloat16),
                pltpu.VMEM((2, out_rows, 2 * width), weight.dtype),
                pltpu.VMEM((2, out_rows, 2 * width), weight.dtype),
                pltpu.VMEM((2, rows, 2 * width), jnp.float32),
                pltpu.VMEM((2, *part), jnp.float32),
                pltpu.SemaphoreType.DMA((2, 2 * NX + 3)),
                pltpu.SemaphoreType.DMA((2, 4)),
            ],
        ),
        out_shape=out_shape,
        input_output_aliases=aliases,
        compiler_params=pltpu.CompilerParams(vmem_limit_bytes=VMEM_LIMIT),
        cost_estimate=pl.CostEstimate(
            flops=2 * total * NX * tok * lhs.shape[0],
            transcendentals=0,
            bytes_accessed=total * (NX * tok * 2 + rows * 4 + out_rows * 4) + lhs.size * 2,
        ),
        name="columns",
    )(info, *operands)


def body(activation, weight, prune_mask, channel_rank):
    tok, block = activation.shape
    chans = weight.shape[1]
    d, r, c = lax.axis_index("dp"), lax.axis_index("row"), lax.axis_index("col")
    y, z = c // NZ, c % NZ
    ncol = NY * NZ
    half = block // 2

    other = send_z(activation)

    everywhere = ("dp", "row", "col")
    per_x = NROW * ncol
    ap = jnp.where((r == 0) & (c == 0), activation[:, :PANEL], jnp.zeros((tok, PANEL), activation.dtype))
    ap = functools.reduce(
        jnp.add, [lax.ppermute(ap, ("row", "col"), [(0, k * NZ)]) for k in range(1, NY)], ap
    )
    ap, other, activation = lax.optimization_barrier((ap, other, activation))
    ap = jnp.concatenate(
        [ap]
        + [
            lax.ppermute(ap, everywhere, [(a * per_x + k * NZ, b * per_x + k * NZ) for a, b in x_perm(s) for k in range(NY)])
            for s in (1, -1, 2)
        ]
    )
    other, ap, activation = lax.optimization_barrier((other, ap, activation))

    first = jnp.stack([activation[:, :half], other[:, :half]])
    second = jnp.stack([activation[:, half:], other[:, half:]])
    first_left, first_right = ring_near(first, send_y)
    second_left, second_right = ring_near(second, send_x)
    ap = ap + lax.ppermute(ap, ("row", "col"), [(i, i + 1) for i in range(0, ncol, NZ)])
    first_left, first_right, second_left, second_right, ap = lax.optimization_barrier(
        (first_left, first_right, second_left, second_right, ap)
    )
    first_far = ring_far(first_left, first_right, send_y)
    second_far = ring_far(second_left, second_right, send_x)
    wp = jnp.where(r == 0, weight[:, :PANEL], jnp.zeros_like(weight[:, :PANEL]))
    both = jnp.concatenate([ap, wp])
    both = both + lax.ppermute(both, "row", [(0, 1)])
    both = both + lax.ppermute(both, "row", [(0, 2), (1, 3)])
    first = (jnp.concatenate([first, first_left]), jnp.concatenate([first_right, *first_far]))
    second = (jnp.concatenate([second, second_left]), jnp.concatenate([second_right, *second_far]))
    first, second, activation = lax.optimization_barrier((first, second, activation))

    first_out, second_out = ring_out(*first, send_x), ring_out(*second, send_y)
    ap, wp = both[: NX * tok].reshape(NX, tok, PANEL), both[NX * tok :]
    corr, panel = panel_step(ap, wp, prune_mask, channel_rank)
    swap = [(i * NROW + j, j * NROW + i) for i in range(NX) for j in range(NROW)]
    own = lax.ppermute(activation, ("dp", "row"), swap)
    first, second, first_out, second_out, corr, own = lax.optimization_barrier(
        (first, second, first_out, second_out, corr, own)
    )
    first_in, second_in = ring_in(*first, send_x), ring_in(*second, send_y)
    own_z = lax.ppermute(own, "row", [(i, i ^ 2) for i in range(NROW)])
    first_out, second_out, first_in, second_in, own, own_z = lax.optimization_barrier(
        (first_out, second_out, first_in, second_in, own, own_z)
    )
    first_far, second_far = ring_out(*first_out, send_x), ring_out(*second_out, send_y)
    core = lax.ppermute(jnp.stack([own, own_z]), "row", [(i, i ^ 1) for i in range(NROW)])
    order = jnp.array([0, 2, 3, 1], jnp.int32)
    lhs = lhs_step(order[((r ^ jnp.arange(NROW)) - d) % NX], own, own_z, core, ap)

    base = jnp.stack([r * chans, (d * ncol + c) * block])
    step = functools.partial(columns_step, base, lhs, corr, panel, weight)

    def place(dy, dz, part):
        return (((y + dy) % NY) * NZ + (z + dz) % NZ) * 2 + part

    def second_entries(shifts):
        return [
            (place(s, dz, 1), [(2 * i + k // 2, (k % 2) * NZ + dz) for k in range(NX)])
            for i, s in enumerate(shifts)
            for dz in range(NZ)
        ]

    def first_entries(skip, ks):
        return [
            (place(s, dz, 0), [(skip + 2 * k + i // 2, (i % 2) * NZ + dz) for k in ks])
            for i, s in enumerate(SHIFTS)
            for dz in range(NZ)
        ]

    far = NX - 1
    pieces = [*second, second_out[0], second_in[0], second_in[1], second_out[1]]
    skip = len(pieces)
    pieces += [*first, first_out[0], first_in[0], first_in[1], first_out[1]]
    entries = second_entries(SHIFTS[:far]) + first_entries(skip, range(far))
    none, slots = [None] * NX, list(range(NX))
    out, hess, parts = step(
        pieces, entries, [0] * 7, [NX] * 3 + [far] * 4, [None] * 7, none[:3] + slots, None, None, None
    )
    entries = second_entries(SHIFTS[far:])
    entries += [(place, [(2 + which, lead)]) for place, ((which, lead),) in first_entries(0, [0])]
    out, hess = step(
        [*second_far, *first_far], entries, [0] + [far] * 4, [NX] * 5, [None] + slots, [None] * 5, parts, out, hess
    )
    return (out, hess)


def solution(mesh):
    return jax.shard_map(
        body,
        mesh=mesh,
        in_specs=(P("dp", ("row", "col")), P(("dp", "col"), "row"), P(("dp", "col"), None), P()),
        out_specs=(P(("dp", "col"), "row"), P(("dp", "col"), "row")),
        check_vma=False,
    )
```

```python
import functools

import jax
import jax.numpy as jnp
from jax import lax
from jax.experimental import pallas as pl
from jax.experimental.pallas import tpu as pltpu
from jax.sharding import PartitionSpec as P

PANEL = 128
KEEP = 8
DAMPING = 0.01

NX = 4
NY = 4
NZ = 2
NROW = 4
VMEM_LIMIT = 28 * 1024 * 1024


def x_perm(k):
    return [(i, (i + k) % NX) for i in range(NX)]


def y_perm(k):
    return [(y * NZ + z, ((y + k) % NY) * NZ + z) for y in range(NY) for z in range(NZ)]


Z_PERM = [(y * NZ + z, y * NZ + 1 - z) for y in range(NY) for z in range(NZ)]


def send_x(a, k):
    return lax.ppermute(a, "dp", x_perm(k))


def send_y(a, k):
    return lax.ppermute(a, "col", y_perm(k))


def send_z(a):
    return lax.ppermute(a, "col", Z_PERM)


SHIFTS = (0, -1, 1, 2)


def ring_near(a, send):
    return send(a, 1), send(a, -1)


def ring_out(a, b, send):
    return send(a, 1), send(b, -1)


def ring_in(a, b, send):
    return send(b, 1), send(a, -1)


def ring_far(left, right, send):
    mid = left.shape[0] // 2
    return send(left[:mid], 1), send(right[mid:], -1)


def panel_kernel(ap_ref, wp_ref, mask_ref, rank_ref, corr_ref, panel_ref):
    hess = jnp.zeros((PANEL, PANEL), jnp.float32)
    for k in range(NX):
        blk = ap_ref[k]
        hess += lax.dot_general(blk, blk, (((0,), (0,)), ((), ())), preferred_element_type=jnp.float32)
    tokens = NX * ap_ref.shape[1]
    row = lax.broadcasted_iota(jnp.int32, (PANEL, PANEL), 0)
    col = lax.broadcasted_iota(jnp.int32, (PANEL, PANEL), 1)
    hess = hess * (2.0 / tokens) + jnp.where(row == col, DAMPING, 0.0)
    lane = lax.broadcasted_iota(jnp.int32, (1, PANEL), 1)
    tiles = [hess[8 * t : 8 * t + 8] for t in range(PANEL // 8)]
    ratio = [None] * PANEL
    for j in reversed(range(PANEL)):
        own = tiles[j // 8][j % 8 : j % 8 + 1]
        r = own / own[:, j : j + 1]
        ratio[j] = jnp.where(lane < j, r, 0.0)
        for t in range((j + 7) // 8):
            tiles[t] = tiles[t] - tiles[t][:, j : j + 1] * r
    ratio_tiles = [jnp.concatenate(ratio[8 * t : 8 * t + 8], axis=0) for t in range(PANEL // 8)]

    keep = jnp.where((mask_ref[...] == 1) | (rank_ref[...] < KEEP), 1.0, 0.0)
    keep_t = keep.T
    w_t = wp_ref[...].astype(jnp.float32).T
    rows = w_t.shape[1]
    acc = [jnp.zeros((8, rows), jnp.float32) for _ in range(PANEL // 8)]
    corr = [None] * PANEL
    for j in range(PANEL):
        c = jnp.where(keep_t[j : j + 1] > 0.5, -acc[j // 8][j % 8 : j % 8 + 1], w_t[j : j + 1])
        corr[j] = c
        for t in range((j + 1) // 8, PANEL // 8):
            acc[t] = acc[t] + ratio_tiles[t][:, j : j + 1] * c
    corr_t = jnp.concatenate(corr, axis=0)
    corr_ref[...] = corr_t.T
    panel_ref[...] = jnp.where(keep_t > 0.5, w_t - corr_t, 0.0).T.astype(panel_ref.dtype)


def panel_step(ap, wp, mask, rank):
    rows = wp.shape[0]
    return pl.pallas_call(
        panel_kernel,
        out_shape=(
            jax.ShapeDtypeStruct((rows, PANEL), jnp.float32),
            jax.ShapeDtypeStruct((rows, PANEL), jnp.bfloat16),
        ),
        compiler_params=pltpu.CompilerParams(vmem_limit_bytes=VMEM_LIMIT),
        cost_estimate=pl.CostEstimate(flops=1 << 33, transcendentals=0, bytes_accessed=1 << 25),
        name="panel_sweep",
    )(ap, wp, mask, rank.reshape(1, PANEL))


def lhs_kernel(block, info, own_ref, own_z_ref, core_ref, ap_ref, lhs_ref):
    tok = own_ref.shape[0]
    for m, piece in enumerate((own_ref, core_ref.at[0], own_z_ref, core_ref.at[1])):
        lhs_ref[:block, pl.ds(pl.multiple_of(info[m] * tok, tok), tok)] = piece[...].T
    for k in range(NX):
        lhs_ref[block:, k * tok : (k + 1) * tok] = ap_ref[k].T


def lhs_step(slots, own, own_z, core, ap):
    tok, block = own.shape
    shape = (block + PANEL, NX * tok)
    whole = pl.BlockSpec(memory_space=pltpu.VMEM)
    return pl.pallas_call(
        functools.partial(lhs_kernel, block),
        out_shape=jax.ShapeDtypeStruct(shape, own.dtype),
        in_specs=[pl.BlockSpec(memory_space=pltpu.SMEM)] + [whole] * 4,
        out_specs=whole,
        compiler_params=pltpu.CompilerParams(vmem_limit_bytes=VMEM_LIMIT),
        cost_estimate=pl.CostEstimate(flops=1 << 31, transcendentals=0, bytes_accessed=1 << 23),
        name="lhs",
    )(slots, own, own_z, core, ap)


def columns_kernel(pairs, tok, width, n_pieces, has_in, has_out, info, lhs_hbm, corr_ref, panel_ref, w_hbm, *rest):
    pieces = rest[:n_pieces]
    part_in = rest[n_pieces] if has_in else None
    lhs_ref, x_buf, w_buf, out_buf, hess_buf, part_buf, lhs_sem, in_sem, out_sem = rest[-9:]
    outs = rest[-12:-9] if has_out else (*rest[-11:-9], None)
    out_hbm, hess_hbm, part_out = outs
    rows = hess_buf.shape[1]
    all_rows = lhs_ref.shape[0]
    scale = 2.0 / (NX * tok)

    def column(p, h):
        return pl.multiple_of(info[2 + 2 * p + h] * width, width)

    def loads(p):
        slot = p % 2
        low, high, places, begin, leave = pairs[p]
        copies = []
        for h in range(2):
            lanes = pl.ds(h * width, width)
            for k in range(high - low):
                which, lead = places[h][k]
                copies.append((pieces[which].at[lead], x_buf.at[slot, pl.ds(k * tok, tok), lanes]))
            if leave is None:
                copies.append((w_hbm.at[:, pl.ds(column(p, h), width)], w_buf.at[slot, :, lanes]))
        if begin is not None:
            copies.append((part_in.at[begin], part_buf.at[slot]))
        return [pltpu.make_async_copy(a, b, in_sem.at[slot, n]) for n, (a, b) in enumerate(copies)]

    def stores(p):
        slot = p % 2
        leave = pairs[p][4]
        copies = []
        if leave is not None:
            copies.append((part_buf.at[slot], part_out.at[leave]))
        else:
            for h in range(2):
                lanes = pl.ds(h * width, width)
                copies.append((hess_buf.at[slot, :, lanes], hess_hbm.at[:, pl.ds(column(p, h), width)]))
                copies.append((out_buf.at[slot, :, lanes], out_hbm.at[:, pl.ds(column(p, h), width)]))
        return [pltpu.make_async_copy(a, b, out_sem.at[slot, n]) for n, (a, b) in enumerate(copies)]

    cut = (NX - 1) * tok
    sides = [
        pltpu.make_async_copy(lhs_hbm.at[:, pl.ds(a, n)], lhs_ref.at[:, pl.ds(a, n)], lhs_sem.at[i])
        for i, (a, n) in enumerate(((0, cut), (cut, tok)))
    ]
    sides[1].start()
    for copy in loads(0):
        copy.start()
    sides[0].start()
    sides[1].wait()
    there = False
    for p in range(len(pairs)):
        slot = p % 2
        low, high, _, begin, leave = pairs[p]
        if low == 0 and not there:
            sides[0].wait()
            there = True
        if p + 1 < len(pairs):
            for copy in loads(p + 1):
                copy.start()
        for copy in loads(p):
            copy.wait()
        if p >= 2:
            for copy in stores(p - 2):
                copy.wait()
        x = x_buf[slot, : (high - low) * tok]
        acc = jnp.dot(lhs_ref[:, low * tok : high * tok], x, preferred_element_type=jnp.float32)
        wide = x.astype(jnp.float32)
        diag = jnp.sum(wide * wide, axis=0, keepdims=True)
        if begin is not None:
            acc = acc + part_buf[slot, :all_rows]
            diag = diag + part_buf[slot, all_rows : all_rows + 1]
        if leave is not None:
            part_buf[slot, :all_rows] = acc
            part_buf[slot, all_rows:] = jnp.broadcast_to(diag, (8, 2 * width))
        else:
            acc = acc * scale
            diag = diag * scale + DAMPING
            change = jnp.dot(
                corr_ref[...],
                acc[rows:] / diag,
                precision=lax.Precision.HIGHEST,
                preferred_element_type=jnp.float32,
            )
            out_buf[slot] = (w_buf[slot].astype(jnp.float32) + change).astype(out_buf.dtype)
            hess_buf[slot] = acc[:rows]
            for h in range(2):
                lanes = slice(h * width, (h + 1) * width)
                col0 = info[0] + column(p, h)
                ahead = col0 - info[1]

                @pl.when((ahead > -width) & (ahead < rows))
                def _():
                    row = lax.broadcasted_iota(jnp.int32, (rows, width), 0)
                    col = lax.broadcasted_iota(jnp.int32, (rows, width), 1)
                    hess_buf[slot, :, lanes] = hess_buf[slot, :, lanes] + jnp.where(row - col == ahead, DAMPING, 0.0)

                @pl.when(col0 == 0)
                def _():
                    out_buf[slot, :, h * width : h * width + PANEL] = panel_ref[...]

        for copy in stores(p):
            copy.start()
    for p in range(max(0, len(pairs) - 2), len(pairs)):
        for copy in stores(p):
            copy.wait()


def columns_step(lhs, corr, panel, weight, info, pieces, entries, low, high, begin, leave, parts, out, hess):
    tok, width = pieces[0].shape[1:]
    out_rows, chans = weight.shape
    rows = lhs.shape[0] - PANEL
    pairs = [
        (low[i], high[i], (entries[2 * i][1], entries[2 * i + 1][1]), begin[i], leave[i])
        for i in range(len(entries) // 2)
    ]
    n_out = sum(a is not None for a in leave)
    fixed = lambda i, info: (0, 0)
    anywhere = pl.BlockSpec(memory_space=pl.ANY)
    operands = [lhs, corr, panel, weight, *pieces]
    if parts is not None:
        operands.append(parts)
    in_specs = [anywhere] + [pl.BlockSpec(a.shape, fixed) for a in (corr, panel)] + [anywhere] * (len(operands) - 3)
    aliases = {}
    if out is not None:
        in_specs += [anywhere] * 2
        operands += [out, hess]
        aliases = {len(operands) - 1: 0, len(operands): 1}
    part = (lhs.shape[0] + 8, 2 * width)
    out_shape = [
        jax.ShapeDtypeStruct((out_rows, chans), weight.dtype),
        jax.ShapeDtypeStruct((rows, chans), jnp.float32),
    ]
    if n_out:
        out_shape.append(jax.ShapeDtypeStruct((n_out, *part), jnp.float32))
    body = functools.partial(columns_kernel, pairs, tok, width, len(pieces), parts is not None, n_out > 0)
    total = len(entries) * width
    return pl.pallas_call(
        body,
        grid_spec=pltpu.PrefetchScalarGridSpec(
            num_scalar_prefetch=1,
            grid=(1,),
            in_specs=in_specs,
            out_specs=[anywhere] * len(out_shape),
            scratch_shapes=[
                pltpu.VMEM(lhs.shape, lhs.dtype),
                pltpu.VMEM((2, NX * tok, 2 * width), jnp.bfloat16),
                pltpu.VMEM((2, out_rows, 2 * width), weight.dtype),
                pltpu.VMEM((2, out_rows, 2 * width), weight.dtype),
                pltpu.VMEM((2, rows, 2 * width), jnp.float32),
                pltpu.VMEM((2, *part), jnp.float32),
                pltpu.SemaphoreType.DMA((2,)),
                pltpu.SemaphoreType.DMA((2, 2 * NX + 3)),
                pltpu.SemaphoreType.DMA((2, 4)),
            ],
        ),
        out_shape=out_shape,
        input_output_aliases=aliases,
        compiler_params=pltpu.CompilerParams(vmem_limit_bytes=VMEM_LIMIT),
        cost_estimate=pl.CostEstimate(
            flops=2 * total * NX * tok * lhs.shape[0],
            transcendentals=0,
            bytes_accessed=total * (NX * tok * 2 + rows * 4 + out_rows * 4) + lhs.size * 2,
        ),
        name="columns",
    )(info, *operands)


def body(activation, weight, prune_mask, channel_rank):
    tok, block = activation.shape
    chans = weight.shape[1]
    d, r, c = lax.axis_index("dp"), lax.axis_index("row"), lax.axis_index("col")
    y, z = c // NZ, c % NZ
    ncol = NY * NZ
    half = block // 2

    base = jnp.stack([r * chans, (d * ncol + c) * block])
    def place(dy, dz, part):
        return (((y + dy) % NY) * NZ + (z + dz) % NZ) * 2 + part

    def second_entries(shifts):
        return [
            (place(s, dz, 1), [(2 * i + k // 2, (k % 2) * NZ + dz) for k in range(NX)])
            for i, s in enumerate(shifts)
            for dz in range(NZ)
        ]

    def first_entries(skip, ks):
        return [
            (place(s, dz, 0), [(skip + 2 * k + i // 2, (i % 2) * NZ + dz) for k in ks])
            for i, s in enumerate(SHIFTS)
            for dz in range(NZ)
        ]

    far = NX - 1
    near_entries = second_entries(SHIFTS[:far]) + first_entries(NX * 2 - 2, range(far))
    far_entries = [
        (place, [(2 + which, lead)]) for place, ((which, lead),) in first_entries(0, [0])
    ] + second_entries(SHIFTS[far:])
    near_info, far_info = (
        jnp.concatenate([base, jnp.stack([place for place, _ in entries])]).astype(jnp.int32)
        for entries in (near_entries, far_entries)
    )
    turn = ((r ^ jnp.arange(NROW)) - d) % NX
    slots = jnp.where(turn == 0, 0, jnp.where(turn == far, 1, turn + 1)).astype(jnp.int32)

    other = send_z(activation)

    ap = jnp.where((r == 0) & (c == 0), activation[:, :PANEL], jnp.zeros((tok, PANEL), activation.dtype))
    ap = functools.reduce(jnp.add, [send_y(ap, k) for k in (1, -1, 2)], ap)
    ap, other, activation = lax.optimization_barrier((ap, other, activation))
    ap = jnp.concatenate([ap] + [send_x(ap, k) for k in (1, -1, 2)])
    other, ap, activation, near_info, far_info, slots = lax.optimization_barrier(
        (other, ap, activation, near_info, far_info, slots)
    )

    first = jnp.stack([activation[:, :half], other[:, :half]])
    second = jnp.stack([activation[:, half:], other[:, half:]])
    first_left, first_right = ring_near(first, send_y)
    second_left, second_right = ring_near(second, send_x)
    ap = ap + lax.ppermute(ap, ("row", "col"), [(i, i + 1) for i in range(0, ncol, NZ)])
    first_left, first_right, second_left, second_right, ap = lax.optimization_barrier(
        (first_left, first_right, second_left, second_right, ap)
    )
    first_far = ring_far(first_left, first_right, send_y)
    second_far = ring_far(second_left, second_right, send_x)
    wp = jnp.where(r == 0, weight[:, :PANEL], jnp.zeros_like(weight[:, :PANEL]))
    both = jnp.concatenate([ap, wp])
    both = both + lax.ppermute(both, "row", [(0, 1)])
    both = both + lax.ppermute(both, "row", [(0, 2), (1, 3)])
    first = (jnp.concatenate([first, first_left]), jnp.concatenate([first_right, *first_far]))
    second = (jnp.concatenate([second, second_left]), jnp.concatenate([second_right, *second_far]))
    first, second, activation = lax.optimization_barrier((first, second, activation))

    first_out, second_out = ring_out(*first, send_x), ring_out(*second, send_y)
    ap, wp = both[: NX * tok].reshape(NX, tok, PANEL), both[NX * tok :]
    corr, panel = panel_step(ap, wp, prune_mask, channel_rank)
    swap = [(i * NROW + j, j * NROW + i) for i in range(NX) for j in range(NROW)]
    own = lax.ppermute(activation, ("dp", "row"), swap)
    first, second, first_out, second_out, corr, own = lax.optimization_barrier(
        (first, second, first_out, second_out, corr, own)
    )
    first_in, second_in = ring_in(*first, send_x), ring_in(*second, send_y)
    own_z = lax.ppermute(own, "row", [(i, i ^ 2) for i in range(NROW)])
    first_out, second_out, first_in, second_in, own, own_z = lax.optimization_barrier(
        (first_out, second_out, first_in, second_in, own, own_z)
    )
    first_far, second_far = ring_out(*first_out, send_x), ring_out(*second_out, send_y)
    core = lax.ppermute(jnp.stack([own, own_z]), "row", [(i, i ^ 1) for i in range(NROW)])
    lhs = lhs_step(slots, own, own_z, core, ap)

    step = functools.partial(columns_step, lhs, corr, panel, weight)
    pieces = [*second, second_out[0], second_in[0], second_in[1], second_out[1]]
    pieces += [*first, first_out[0], first_in[0], first_in[1], first_out[1]]
    none, parts = [None] * NX, list(range(NX))
    out, hess, sums = step(
        near_info, pieces, near_entries, [0] * 7, [NX] * 3 + [far] * 4, [None] * 7, none[:3] + parts, None, None, None
    )
    out, hess = step(
        far_info,
        [*second_far, *first_far],
        far_entries,
        [far] * 4 + [0],
        [NX] * 5,
        parts + [None],
        [None] * 5,
        sums,
        out,
        hess,
    )
    return (out, hess)


def solution(mesh):
    return jax.shard_map(
        body,
        mesh=mesh,
        in_specs=(P("dp", ("row", "col")), P(("dp", "col"), "row"), P(("dp", "col"), None), P()),
        out_specs=(P(("dp", "col"), "row"), P(("dp", "col"), "row")),
        check_vma=False,
    )
```
